32 devices in a mesh: groups: 2 (over x), expert: 16 (over z, y, core).
Axes of the slice: x: 2, y: 2, z: 4, core: 2. Of those that a mesh axis runs over, the one named last changes fastest.
Arguments:
- hidden_states: bfloat16 [2, 512, 4096], P(None, ('groups', 'expert')), parts along dimension 1, may hold values from -6 to 6
- expert_ids: int32 [2, 512, 8], P(None, ('groups', 'expert')), parts along dimension 1, may hold values from 0 to 15, all different within a row; in each aligned block of 16 rows (0 to 15, 16 to 31, ..., all dimensions but the last counted through in order) at most 16 rows name the same one
- router_probs: float32 [2, 512, 8], P(None, ('groups', 'expert')), parts along dimension 1, may hold values from 0.05 to 1
- swap_flags: int32 [16], replicated, may hold values from 0 to 1, as said below
- w_gate: bfloat16 [16, 4096, 768], P('expert'), may hold values from -0.09375 to 0.09375
- w_up: bfloat16 [16, 4096, 768], P('expert'), may hold values from -0.09375 to 0.09375
- w_down: bfloat16 [16, 768, 4096], P('expert'), may hold values from -0.21875 to 0.21875
Outputs:
- mixed: bfloat16 [2, 512, 4096], P(None, ('groups', 'expert')), parts along dimension 1
The draws below stay inside these ranges and needn't reach their ends.
There are 2 independent parts, one for each index of `groups`. The reference program is written for one: setup_inputs(seed, part) draws one part's arguments, and reference() takes and returns one part's arrays. A program takes and returns all parts, laid end to end along the dimension named above; an argument that names none is the same for every part. Nothing has to cross between parts.
Inputs may be any that keep to these rules, and one draw needn't show every extreme that they name: `expert_ids`: within one step, the 16 rows of one device (aligned blocks of 16 rows) name any one slot at most 16 times, a bound that some block reaches; the 8 ids of a row differ. swap_flags[e] equals swap_flags[e XOR 1] for every slot e.
All inputs are finite; a program needn't handle non-finite values.
Results may differ from the reference program's by a relative error of at most 0.0058.
Values may be sent and summed in bfloat16 or wider, within the bound.
A program may use at most 128 MiB of HBM per device.

```python
import math
import jax
import jax.numpy as jnp
import numpy as np
from jax import lax

D = 4096
FW = 768
TOPK = 8
STEPS = 2
TOK_DEV = 16
EXPERTS = 16
TOKENS = 256
CAP = 16
N_EXPERT = 16


def draw_swap_flags(key, part):
    pair_flags = jax.random.randint(jax.random.fold_in(key, 7), (EXPERTS // 2,), 0, 2).astype(jnp.int32)
    return jnp.repeat(pair_flags, 2).astype(jnp.int32)


def block_scale(own_key, shape, shards, low, high):
    level, own = 1.0, jax.random.fold_in(own_key, 6)
    for dim, parts in shards:
        steps = jnp.exp(jax.random.uniform(jax.random.fold_in(own, dim), (parts,), jnp.float32, low / len(shards), high / len(shards)))
        level = level * jnp.repeat(steps, shape[dim] // parts).reshape([-1 if axis == dim else 1 for axis in range(len(shape))])
    return level


def routed_block(own_key, own, number, rows, number_of, top, bound, skew):
    sequence = jax.random.permutation(own_key, number_of)
    crowded, usual = load_shares(number_of, rows * top, bound, skew, True), load_shares(number_of, rows * top, bound, skew, False)
    places = jnp.arange(number_of)

    def named(tallies, offset_by):
        used = int((tallies > 0).sum())
        fixed = max(1, used // 4)
        shifted = fixed + (places - fixed + offset_by * (used - fixed)) % max(1, number_of - fixed)
        return jnp.zeros((number_of,), jnp.int32).at[sequence[jnp.where(places < fixed, places, shifted)]].set(jnp.asarray(tallies, jnp.int32))

    tallies = jnp.where(number % 4 == 0, named(crowded, number // 4), named(usual, number - number // 4 - 1))
    mixed = jax.random.permutation(jax.random.fold_in(own, 3), number_of)
    source_of, taker = mixed[0:number_of // 2 * 2:2], mixed[1:number_of // 2 * 2:2]
    margin = jnp.minimum(tallies[source_of] - 1, bound - tallies[taker]) // 2
    margin = jnp.where((source_of == sequence[0]) | (taker == sequence[0]) | (tallies[taker] == 0), 0, jnp.maximum(margin, 0))
    shifted = jax.random.randint(jax.random.fold_in(own, 4), (number_of // 2,), 0, 1 << 20) % (margin + 1)
    tallies = tallies.at[source_of].add(-shifted).at[taker].add(shifted)
    members = jnp.searchsorted(jnp.cumsum(tallies), jnp.arange(rows * top), side="right").astype(jnp.int32)
    listing = members.reshape(top, rows).T
    listing = listing[jax.random.permutation(jax.random.fold_in(own, 1), rows)]
    offset_by = jax.random.randint(jax.random.fold_in(own, 2), (rows, 1), 0, top)
    return jnp.take_along_axis(listing, (jnp.arange(top)[None, :] + offset_by) % top, axis=1)


def load_shares(number_of, total, bound, slope, full):
    portions = [(1 << 20) // math.isqrt(grade ** slope) + 1 for grade in range(1, number_of + 1)]
    largest = bound if full else min(bound, max(-(-total // number_of), total * portions[0] // sum(portions)))
    least = 1 if total - largest >= number_of - 1 else 0
    holding, spare = [largest] + [least] * (number_of - 1), total - largest - least * (number_of - 1)
    while spare > 0:
        movable = [i for i in range(1, number_of) if holding[i] < largest] or [i for i in range(1, number_of) if holding[i] < bound]
        whole, budget = sum([portions[i] for i in movable]), spare
        for i in movable:
            more = min(bound - holding[i], max(1, budget * portions[i] // whole), spare)
            holding[i] = holding[i] + more
            spare = spare - more
    return np.array(holding)


def scatter_about(rng, extent, scale, bound, pieces=(), kind=jnp.bfloat16):
    entries = scale * jax.random.normal(rng, extent, jnp.float32)
    if pieces:
        entries = entries * block_scale(rng, extent, pieces, -0.22, 0.18)
    return jnp.clip(entries, -bound, bound).astype(kind)


def setup_inputs(seed: int = 0, part: int = 0) -> dict:
    key_list = jax.random.split(jax.random.key(seed), 8)
    part_keys = jax.random.split(jax.random.fold_in(key_list[7], part), 8)
    hidden_states = scatter_about(part_keys[0], (STEPS, TOKENS, D), 1.0, 6.0, ((1, 16),))
    expert_ids_keys = jax.random.split(jax.random.fold_in(part_keys[1], 1), STEPS * TOKENS // TOK_DEV)
    expert_ids_turns = jax.random.permutation(jax.random.fold_in(part_keys[1], 3), STEPS * TOKENS // TOK_DEV)
    expert_ids = jax.vmap(lambda own, number: routed_block(jax.random.fold_in(part_keys[1], 2), own, number, TOK_DEV, EXPERTS, TOPK, CAP, 2))(expert_ids_keys, expert_ids_turns).reshape((STEPS, TOKENS, TOPK))
    router_probs = jnp.clip(jnp.exp(math.log(1.0) - 2.9957323 * jax.random.uniform(part_keys[2], (STEPS, TOKENS, TOPK), jnp.float32) ** block_scale(part_keys[2], (STEPS, TOKENS, TOPK), ((1, 16),), -0.2, 0.2)), 0.05, 1.0)
    swap_flags = draw_swap_flags(jax.random.fold_in(key_list[7], 71), part)
    w_gate = scatter_about(key_list[4], (EXPERTS, D, FW), D ** -0.5, 0.09375, ((0, 16),))
    w_up = scatter_about(key_list[5], (EXPERTS, D, FW), D ** -0.5, 0.09375, ((0, 16),))
    w_down = scatter_about(key_list[6], (EXPERTS, FW, D), FW ** -0.5, 0.21875, ((0, 16),))
    return {"hidden_states": hidden_states, "expert_ids": expert_ids, "router_probs": router_probs, "swap_flags": swap_flags, "w_gate": w_gate, "w_up": w_up, "w_down": w_down}


def expert_mlp(rows, gate_matrix, up_matrix, down_matrix):
    gate = jnp.dot(rows, gate_matrix, preferred_element_type=jnp.float32)
    up_part = jnp.dot(rows, up_matrix, preferred_element_type=jnp.float32)
    hidden = (jax.nn.silu(gate) * up_part).astype(jnp.bfloat16)
    return jnp.dot(hidden, down_matrix, preferred_element_type=jnp.float32).astype(jnp.bfloat16)


def apply_expert(operands):
    return expert_mlp(operands[0], operands[1], operands[2], operands[3])


def reference(hidden_states, expert_ids, router_probs, swap_flags, w_gate, w_up, w_down):
    outputs = []
    slots_iota = jnp.arange(EXPERTS, dtype=jnp.int32)
    partner = jnp.bitwise_xor(slots_iota, 1).astype(jnp.int32)
    for step_index in range(STEPS):
        if step_index == 0:
            held = slots_iota
        else:
            held = jnp.where(swap_flags == 1, partner, slots_iota).astype(jnp.int32)
        states = hidden_states[step_index]
        routed = expert_ids[step_index]
        weights_raw = router_probs[step_index]
        shares = weights_raw / jnp.sum(weights_raw, axis=-1, keepdims=True)
        blocks = routed.reshape(N_EXPERT, TOK_DEV * TOPK)
        onehot = (blocks[:, :, None] == slots_iota[None, None, :]).astype(jnp.int32)
        before = (jnp.cumsum(onehot, axis=1).astype(jnp.int32) - onehot) * onehot
        slot_rank = jnp.sum(before, axis=2).astype(jnp.int32)
        source = jnp.arange(N_EXPERT, dtype=jnp.int32)[:, None]
        target = (blocks * (N_EXPERT * CAP) + source * CAP + slot_rank).reshape(-1).astype(jnp.int32)
        token_row = (source * TOK_DEV + jnp.arange(TOK_DEV * TOPK, dtype=jnp.int32)[None, :] // TOPK).reshape(-1).astype(jnp.int32)
        row_table = jnp.full((EXPERTS * N_EXPERT * CAP,), TOKENS, jnp.int32).at[target].set(token_row)
        padded = jnp.concatenate([states, jnp.zeros((1, D), jnp.bfloat16)], axis=0)
        gathered = padded[row_table].reshape(EXPERTS, N_EXPERT * CAP, D)
        results = lax.map(apply_expert, (gathered, w_gate[held], w_up[held], w_down[held]))
        picked = results.reshape(-1, D)[target].reshape(TOKENS, TOPK, D).astype(jnp.float32)
        outputs.append(jnp.sum(shares[:, :, None] * picked, axis=1).astype(jnp.bfloat16))
    return jnp.stack(outputs)
```

```python
import functools

import jax
import jax.numpy as jnp
from jax import lax
from jax.experimental import pallas as pl
from jax.experimental.pallas import tpu as pltpu
from jax.sharding import PartitionSpec as P

MESH = pl.DeviceIdType.MESH
CHUNKS = 4
F32 = jnp.float32
BF16 = jnp.bfloat16


def moe_kernel(
    n, x_ref, coef_ref, wg_hbm, wu_hbm, wd_hbm, out_ref,
    tok, coef, wg, wu, wd, acc_g, acc_u, hid, part, r1, q, r2, w, r3,
    z_send, z_recv, y_send, y_recv, s_send, s_recv, c_send, c_recv,
    r1_send, r1_recv, r2_send, r2_recv, r3_send, r3_recv, w_sem, own_sem,
):
    nz = n // 4
    steps, rows, width = x_ref.shape
    dc = width // CHUNKS
    units = steps * CHUNKS
    me = lax.axis_index("expert")
    k = lax.rem(me, 2)
    y = lax.rem(lax.div(me, 2), 2)
    z = lax.div(me, 4)
    ok, oy = 1 - k, 1 - y

    def zat(d):
        return lax.rem(z + d + nz, nz)

    def dev(zz, yy, kk):
        return {"expert": zz * 4 + yy * 2 + kk}

    def remote(src, dst, ss, rs, target):
        return pltpu.make_async_remote_copy(
            src_ref=src, dst_ref=dst, send_sem=ss, recv_sem=rs,
            device_id=target, device_id_type=MESH,
        )

    sib = dev(z, y, ok)
    ynb = dev(z, oy, k)

    wcopies = {}
    for c in range(CHUNKS):
        part_rows = pl.ds(c * dc, dc)
        wcopies["g", c] = pltpu.make_async_copy(wg_hbm.at[0, part_rows], wg.at[part_rows], w_sem.at[0, c])
        wcopies["u", c] = pltpu.make_async_copy(wu_hbm.at[0, part_rows], wu.at[part_rows], w_sem.at[1, c])
        wcopies["d", c] = pltpu.make_async_copy(wd_hbm.at[0, :, part_rows], wd.at[:, part_rows], w_sem.at[2, c])

    barrier = pltpu.get_barrier_semaphore()
    for d in range(1, n):
        pl.semaphore_signal(
            barrier, inc=1, device_id={"expert": lax.rem(me + d, n)}, device_id_type=MESH
        )
    for name in ("g", "u"):
        wcopies[name, 0].start()
    own = pltpu.make_async_copy(x_ref, tok.at[:, k, y, z], own_sem)
    own.start()
    pl.semaphore_wait(barrier, n - 1)

    def cols(u):
        return u // CHUNKS, pl.ds((u % CHUNKS) * dc, dc)

    def xs(u):
        s, cc = cols(u)
        return x_ref.at[s, :, cc]

    def slot(u, kk, yy, zz):
        s, cc = cols(u)
        return tok.at[s, kk, yy, zz, :, cc]

    def column(u, kk, yy):
        s, cc = cols(u)
        return tok.at[s, kk, yy, :, :, cc]

    sends = []

    def send(copy):
        copy.start()
        sends.append(copy)

    def ag1(u):
        for d in range(1, nz):
            send(remote(xs(u), slot(u, k, y, z), z_send.at[u, d - 1], z_recv.at[u, d - 1], dev(zat(d), y, k)))

    def ag2(u):
        send(remote(xs(u), slot(u, k, y, z), y_send.at[u, 0], y_recv.at[u, 0], ynb))
        for d in range(1, nz):
            here = slot(u, k, y, zat(-d))
            remote(here, here, z_send.at[u, d - 1], z_recv.at[u, d - 1], sib).wait_recv()
            send(remote(here, here, y_send.at[u, d], y_recv.at[u, d], ynb))
        col = column(u, k, y)
        send(remote(col, col, s_send.at[u, 0], s_recv.at[u, 0], sib))

    def ag3(u):
        for d in range(nz):
            here = slot(u, k, oy, zat(-d))
            remote(here, here, y_send.at[u, d], y_recv.at[u, d], ynb).wait_recv()
        col = column(u, k, oy)
        send(remote(col, col, s_send.at[u, 1], s_recv.at[u, 1], sib))

    def ag4(u):
        for i, yy in enumerate((y, oy)):
            col = column(u, ok, yy)
            remote(col, col, s_send.at[u, i], s_recv.at[u, i], sib).wait_recv()

    def gate_up(u):
        s, cc = cols(u)
        c = u % CHUNKS
        if s == 0:
            wcopies["g", c].wait()
            wcopies["u", c].wait()
        lhs = tok[s, :, :, :, :, cc].reshape(n * rows, dc)
        g = jnp.dot(lhs, wg[cc, :], preferred_element_type=F32)
        up = jnp.dot(lhs, wu[cc, :], preferred_element_type=F32)
        if c > 0:
            g = acc_g[...] + g
            up = acc_u[...] + up
        if c < CHUNKS - 1:
            acc_g[...] = g
            acc_u[...] = up
        else:
            hid[...] = (g / (1.0 + jnp.exp(-g)) * up).astype(BF16)

    def share_column(s):
        table = coef[...].reshape(n, 1, 128)
        spread = jnp.broadcast_to(table, (n, rows, 128)).reshape(n * rows, 128)
        lane = lax.broadcasted_iota(jnp.int32, (n * rows, 128), 1)
        token = lax.rem(lax.broadcasted_iota(jnp.int32, (n * rows, 128), 0), rows)
        return jnp.sum(jnp.where(lane == token + s * rows, spread, 0.0), axis=1, keepdims=True)

    def down(u):
        s, cc = cols(u)
        if s == 0:
            wcopies["d", u % CHUNKS].wait()
        res = jnp.dot(hid[...], wd[:, cc], preferred_element_type=F32)
        part[u] = (res * share_column(s)).astype(BF16).reshape(2, 2, nz, rows, dc)
        send(remote(part.at[u, ok], r1.at[u], r1_send.at[u], r1_recv.at[u], sib))

    def rs2(u):
        remote(r1.at[u], r1.at[u], r1_send.at[u], r1_recv.at[u], sib).wait_recv()
        q[u] = (part[u, k, oy].astype(F32) + r1[u, oy].astype(F32)).astype(BF16)
        send(remote(q.at[u], r2.at[u], r2_send.at[u], r2_recv.at[u], ynb))

    def rs3(u):
        remote(r2.at[u], r2.at[u], r2_send.at[u], r2_recv.at[u], ynb).wait_recv()
        total = part[u, k, y].astype(F32) + r1[u, y].astype(F32) + r2[u].astype(F32)
        w[u] = total.astype(BF16)
        for d in range(1, nz):
            send(remote(w.at[u, zat(d)], r3.at[u, d - 1], r3_send.at[u, d - 1], r3_recv.at[u, d - 1], dev(zat(d), y, k)))

    def rs4(u):
        s, cc = cols(u)
        total = part[u, k, y, z].astype(F32) + r1[u, y, z].astype(F32) + r2[u, z].astype(F32)
        for d in range(1, nz):
            here = r3.at[u, d - 1]
            remote(here, here, r3_send.at[u, d - 1], r3_recv.at[u, d - 1], sib).wait_recv()
            total = total + r3[u, d - 1].astype(F32)
        out_ref[s, :, cc] = total.astype(BF16)

    ag1(0)
    place = k * (2 * nz) + y * nz + z
    for d in range(1, n):
        to = lax.rem(me + d, n)
        send(remote(coef_ref.at[to], coef.at[place], c_send.at[d - 1], c_recv.at[d - 1], {"expert": to}))
    coef[place] = coef_ref[me]
    for u in range(1, units):
        ag1(u)
    for c in range(1, CHUNKS):
        wcopies["g", c].start()
        wcopies["u", c].start()
    for c in range(CHUNKS):
        wcopies["d", c].start()
    own.wait()

    down_at = {}
    for s in range(steps):
        for c in range(CHUNKS):
            down_at[s * CHUNKS + c] = (s + 1) * CHUNKS + 1 + (c + 1 if s < steps - 1 else c)
    last = max(down_at.values()) + 3
    coef_done = False
    for t in range(last + 1):
        if t < units:
            ag2(t)
        if 0 <= t - 1 < units:
            ag3(t - 1)
        for stage, fn in ((1, rs2), (2, rs3), (3, rs4)):
            for u in range(units):
                if down_at[u] + stage == t:
                    fn(u)
        for u in range(units):
            if down_at[u] == t and u < units - CHUNKS:
                down(u)
        if 0 <= t - 2 < units:
            if not coef_done:
                coef_done = True
                for d in range(1, n):
                    src = lax.rem(me + n - d, n)
                    at = lax.rem(src, 2) * (2 * nz) + lax.rem(lax.div(src, 2), 2) * nz + lax.div(src, 4)
                    here = coef.at[at]
                    remote(here, here, c_send.at[d - 1], c_recv.at[d - 1], sib).wait_recv()
            ag4(t - 2)
            gate_up(t - 2)
        for u in range(units):
            if down_at[u] == t and u >= units - CHUNKS:
                down(u)
    for copy in sends:
        copy.wait_send()


def moe(n, x, coef, wg, wu, wd):
    steps, rows, width = x.shape
    hidden = wg.shape[2]
    nz = n // 4
    dc = width // CHUNKS
    units = steps * CHUNKS
    vm = pltpu.VMEM
    dma = pltpu.SemaphoreType.DMA
    vspec = pl.BlockSpec(memory_space=pltpu.VMEM)
    hspec = pl.BlockSpec(memory_space=pl.ANY)
    return pl.pallas_call(
        functools.partial(moe_kernel, n),
        out_shape=jax.ShapeDtypeStruct(x.shape, BF16),
        in_specs=[vspec, vspec, hspec, hspec, hspec],
        out_specs=vspec,
        scratch_shapes=[
            vm((steps, 2, 2, nz, rows, width), BF16),
            vm((n, 1, 128), F32),
            vm((width, hidden), BF16),
            vm((width, hidden), BF16),
            vm((hidden, width), BF16),
            vm((n * rows, hidden), F32),
            vm((n * rows, hidden), F32),
            vm((n * rows, hidden), BF16),
            vm((units, 2, 2, nz, rows, dc), BF16),
            vm((units, 2, nz, rows, dc), BF16),
            vm((units, nz, rows, dc), BF16),
            vm((units, nz, rows, dc), BF16),
            vm((units, nz, rows, dc), BF16),
            vm((units, nz - 1, rows, dc), BF16),
            dma((units, nz - 1)), dma((units, nz - 1)),
            dma((units, nz)), dma((units, nz)),
            dma((units, 2)), dma((units, 2)),
            dma((n - 1,)), dma((n - 1,)),
            dma((units,)), dma((units,)),
            dma((units,)), dma((units,)),
            dma((units, nz - 1)), dma((units, nz - 1)),
            dma((3, CHUNKS)), dma,
        ],
        compiler_params=pltpu.CompilerParams(
            collective_id=0, has_side_effects=True, vmem_limit_bytes=67000000
        ),
    )(x, coef, wg, wu, wd)


def on_device(hidden_states, expert_ids, router_probs, swap_flags, w_gate, w_up, w_down):
    n = lax.axis_size("expert")
    steps, rows, _ = hidden_states.shape
    shares = router_probs / jnp.sum(router_probs, axis=-1, keepdims=True)
    experts = jnp.arange(n, dtype=jnp.int32)
    later = jnp.where(swap_flags == 1, jnp.bitwise_xor(experts, 1), experts)
    step_of = jnp.arange(steps, dtype=jnp.int32)[:, None]
    served = jnp.where(step_of == 0, experts[None, :], later[None, :])
    match = expert_ids[None] == served.T[:, :, None, None]
    coef = jnp.sum(jnp.where(match, shares[None], 0.0), axis=-1).reshape(n, 1, steps * rows)
    coef = jnp.pad(coef, ((0, 0), (0, 0), (0, 128 - steps * rows)))
    return moe(n, hidden_states, coef, w_gate, w_up, w_down)


def solution(mesh):
    return jax.shard_map(
        on_device,
        mesh=mesh,
        in_specs=(
            P(None, ("groups", "expert"), None),
            P(None, ("groups", "expert"), None),
            P(None, ("groups", "expert"), None),
            P(),
            P("expert", None, None),
            P("expert", None, None),
            P("expert", None, None),
        ),
        out_specs=P(None, ("groups", "expert"), None),
        check_vma=False,
    )
```

```python
import functools

import jax
import jax.numpy as jnp
from jax import lax
from jax.experimental import pallas as pl
from jax.experimental.pallas import tpu as pltpu
from jax.sharding import PartitionSpec as P

MESH = pl.DeviceIdType.MESH
CHUNKS = 4
F32 = jnp.float32
BF16 = jnp.bfloat16


def moe_kernel(
    n, x_ref, ids_ref, probs_ref, flag_ref, wg_hbm, wu_hbm, wd_hbm, out_ref,
    tok, coef_ref, coef, wg, wu, wd, acc_g, acc_u, hid, part, r1, q, r2, w, r3,
    z_send, z_recv, y_send, y_recv, s_send, s_recv, c_send, c_recv,
    r1_send, r1_recv, r2_send, r2_recv, r3_send, r3_recv, w_sem, own_sem,
):
    nz = n // 4
    steps, rows, width = x_ref.shape
    dc = width // CHUNKS
    units = steps * CHUNKS
    me = lax.axis_index("expert")
    k = lax.rem(me, 2)
    y = lax.rem(lax.div(me, 2), 2)
    z = lax.div(me, 4)
    ok, oy = 1 - k, 1 - y

    def zat(d):
        return lax.rem(z + d + nz, nz)

    def dev(zz, yy, kk):
        return {"expert": zz * 4 + yy * 2 + kk}

    def remote(src, dst, ss, rs, target):
        return pltpu.make_async_remote_copy(
            src_ref=src, dst_ref=dst, send_sem=ss, recv_sem=rs,
            device_id=target, device_id_type=MESH,
        )

    sib = dev(z, y, ok)
    ynb = dev(z, oy, k)

    wcopies = {}
    for c in range(CHUNKS):
        part_rows = pl.ds(c * dc, dc)
        wcopies["g", c] = pltpu.make_async_copy(wg_hbm.at[0, part_rows], wg.at[part_rows], w_sem.at[0, c])
        wcopies["u", c] = pltpu.make_async_copy(wu_hbm.at[0, part_rows], wu.at[part_rows], w_sem.at[1, c])
        wcopies["d", c] = pltpu.make_async_copy(wd_hbm.at[0, :, part_rows], wd.at[:, part_rows], w_sem.at[2, c])

    barrier = pltpu.get_barrier_semaphore()
    for d in range(1, n):
        pl.semaphore_signal(
            barrier, inc=1, device_id={"expert": lax.rem(me + d, n)}, device_id_type=MESH
        )
    for name in ("g", "u"):
        wcopies[name, 0].start()
    own = pltpu.make_async_copy(x_ref, tok.at[:, k, y, z], own_sem)
    own.start()

    lane = lax.broadcasted_iota(jnp.int32, (rows, 128), 1)
    flags = jnp.zeros((rows, 128), jnp.int32)
    for e in range(n):
        flags = jnp.where(lane == e, flag_ref[e], flags)
    tables = []
    for s in range(steps):
        served = lane if s == 0 else jnp.where(flags == 1, jnp.bitwise_xor(lane, 1), lane)
        ids, probs = ids_ref[s], probs_ref[s]
        shares = probs / jnp.sum(probs, axis=1, keepdims=True)
        table = jnp.zeros((rows, 128), F32)
        for j in range(ids.shape[1]):
            table = jnp.where(ids[:, j : j + 1] == served, shares[:, j : j + 1], table)
        tables.append(table)
    tables.append(jnp.zeros((128 - steps * rows, 128), F32))
    flipped = jnp.transpose(jnp.concatenate(tables, axis=0))
    for e in range(n):
        coef_ref[e] = flipped[e : e + 1]
    pl.semaphore_wait(barrier, n - 1)

    def cols(u):
        return u // CHUNKS, pl.ds((u % CHUNKS) * dc, dc)

    def xs(u):
        s, cc = cols(u)
        return x_ref.at[s, :, cc]

    def slot(u, kk, yy, zz):
        s, cc = cols(u)
        return tok.at[s, kk, yy, zz, :, cc]

    def column(u, kk, yy):
        s, cc = cols(u)
        return tok.at[s, kk, yy, :, :, cc]

    sends = []

    def send(copy):
        copy.start()
        sends.append(copy)

    def ag1(u):
        for d in range(1, nz):
            send(remote(xs(u), slot(u, k, y, z), z_send.at[u, d - 1], z_recv.at[u, d - 1], dev(zat(d), y, k)))
        send(remote(xs(u), slot(u, k, y, z), y_send.at[u, 0], y_recv.at[u, 0], ynb))

    def ag2(u):
        for d in range(1, nz):
            here = slot(u, k, y, zat(-d))
            remote(here, here, z_send.at[u, d - 1], z_recv.at[u, d - 1], sib).wait_recv()
            send(remote(here, here, y_send.at[u, d], y_recv.at[u, d], ynb))
        col = column(u, k, y)
        send(remote(col, col, s_send.at[u, 0], s_recv.at[u, 0], sib))

    def ag3(u):
        for d in range(nz):
            here = slot(u, k, oy, zat(-d))
            remote(here, here, y_send.at[u, d], y_recv.at[u, d], ynb).wait_recv()
        col = column(u, k, oy)
        send(remote(col, col, s_send.at[u, 1], s_recv.at[u, 1], sib))

    def ag4(u):
        for i, yy in enumerate((y, oy)):
            col = column(u, ok, yy)
            remote(col, col, s_send.at[u, i], s_recv.at[u, i], sib).wait_recv()

    def gate_up(u):
        s, cc = cols(u)
        c = u % CHUNKS
        if s == 0:
            wcopies["g", c].wait()
            wcopies["u", c].wait()
        lhs = tok[s, :, :, :, :, cc].reshape(n * rows, dc)
        g = jnp.dot(lhs, wg[cc, :], preferred_element_type=F32)
        up = jnp.dot(lhs, wu[cc, :], preferred_element_type=F32)
        if c > 0:
            g = acc_g[...] + g
            up = acc_u[...] + up
        if c < CHUNKS - 1:
            acc_g[...] = g
            acc_u[...] = up
        else:
            hid[...] = (g / (1.0 + jnp.exp(-g)) * up).astype(BF16)

    def share_column(s):
        table = coef[...].reshape(n, 1, 128)
        spread = jnp.broadcast_to(table, (n, rows, 128)).reshape(n * rows, 128)
        lane = lax.broadcasted_iota(jnp.int32, (n * rows, 128), 1)
        token = lax.rem(lax.broadcasted_iota(jnp.int32, (n * rows, 128), 0), rows)
        return jnp.sum(jnp.where(lane == token + s * rows, spread, 0.0), axis=1, keepdims=True)

    def down(u):
        s, cc = cols(u)
        if s == 0:
            wcopies["d", u % CHUNKS].wait()
        res = jnp.dot(hid[...], wd[:, cc], preferred_element_type=F32)
        part[u] = (res * share_column(s)).astype(BF16).reshape(2, 2, nz, rows, dc)
        send(remote(part.at[u, ok], r1.at[u], r1_send.at[u], r1_recv.at[u], sib))

    def y_back(u, d):
        zz = zat(d)
        return remote(q.at[u, zz], r2.at[u, zz], r2_send.at[u, d], r2_recv.at[u, d], ynb)

    def rs2(u):
        remote(r1.at[u], r1.at[u], r1_send.at[u], r1_recv.at[u], sib).wait_recv()
        q[u] = (part[u, k, oy].astype(F32) + r1[u, oy].astype(F32)).astype(BF16)
        for d in range(1, nz):
            send(y_back(u, d))

    def rs2_own(u):
        send(y_back(u, 0))

    def column_sum(u, zz):
        return part[u, k, y, zz].astype(F32) + r1[u, y, zz].astype(F32) + r2[u, zz].astype(F32)

    def rs3(u):
        for d in range(1, nz):
            zz = zat(d)
            y_back(u, d).wait_recv()
            w[u, zz] = column_sum(u, zz).astype(BF16)
            send(remote(w.at[u, zz], r3.at[u, d - 1], r3_send.at[u, d - 1], r3_recv.at[u, d - 1], dev(zz, y, k)))

    def rs4(u):
        s, cc = cols(u)
        y_back(u, 0).wait_recv()
        total = column_sum(u, z)
        for d in range(1, nz):
            here = r3.at[u, d - 1]
            remote(here, here, r3_send.at[u, d - 1], r3_recv.at[u, d - 1], sib).wait_recv()
            total = total + r3[u, d - 1].astype(F32)
        out_ref[s, :, cc] = total.astype(BF16)

    ag1(0)
    place = k * (2 * nz) + y * nz + z
    for d in range(1, n):
        to = lax.rem(me + d, n)
        send(remote(coef_ref.at[to], coef.at[place], c_send.at[d - 1], c_recv.at[d - 1], {"expert": to}))
    coef[place] = coef_ref[me]
    for u in range(1, 2):
        ag1(u)
    for c in range(1, CHUNKS):
        wcopies["g", c].start()
        wcopies["u", c].start()
    for c in range(CHUNKS):
        wcopies["d", c].start()
    own.wait()

    def coef_wait():
        for d in range(1, n):
            src = lax.rem(me + n - d, n)
            at = lax.rem(src, 2) * (2 * nz) + lax.rem(lax.div(src, 2), 2) * nz + lax.div(src, 4)
            here = coef.at[at]
            remote(here, here, c_send.at[d - 1], c_recv.at[d - 1], sib).wait_recv()

    after = {}
    for s in range(steps - 1):
        base, first = (s + 1) * CHUNKS + 1, s * CHUNKS
        half = CHUNKS // 2
        for c in range(CHUNKS):
            late = c // half
            after.setdefault(base + late, []).append((down, first + c))
        for c in range(CHUNKS):
            late = c // half
            after.setdefault(base + 1 + late, []).extend([(rs2, first + c), (rs2_own, first + c)])
        for c in range(half):
            after.setdefault(base + 3, []).append((rs3, first + c))
    for t in range(units + 2):
        if t < units:
            ag2(t)
            if t + 2 < units:
                ag1(t + 2)
        if 0 <= t - 1 < units:
            ag3(t - 1)
        if t == 2:
            coef_wait()
        if t >= 2:
            ag4(t - 2)
            gate_up(t - 2)
        for fn, u in after.get(t, ()):
            fn(u)
    tail = units - CHUNKS
    held_back = [u for s in range(steps - 1) for u in range(s * CHUNKS + CHUNKS // 2, (s + 1) * CHUNKS)]
    for c in range(CHUNKS + 2):
        if c < CHUNKS:
            down(tail + c)
        for u in held_back[:1]:
            rs3(u)
        held_back = held_back[1:]
        if 0 <= c - 1 < CHUNKS:
            rs2(tail + c - 1)
        if c == CHUNKS:
            for u in range(tail, units):
                rs2_own(u)
        if 0 <= c - 2 < CHUNKS:
            rs3(tail + c - 2)
    for u in held_back:
        rs3(u)
    for u in range(units):
        rs4(u)
    for copy in sends:
        copy.wait_send()


def moe(n, x, ids, probs, flags, wg, wu, wd):
    steps, rows, width = x.shape
    hidden = wg.shape[2]
    nz = n // 4
    dc = width // CHUNKS
    units = steps * CHUNKS
    vm = pltpu.VMEM
    dma = pltpu.SemaphoreType.DMA
    vspec = pl.BlockSpec(memory_space=pltpu.VMEM)
    hspec = pl.BlockSpec(memory_space=pl.ANY)
    return pl.pallas_call(
        functools.partial(moe_kernel, n),
        out_shape=jax.ShapeDtypeStruct(x.shape, BF16),
        in_specs=[vspec, vspec, vspec, pl.BlockSpec(memory_space=pltpu.SMEM), hspec, hspec, hspec],
        out_specs=vspec,
        scratch_shapes=[
            vm((steps, 2, 2, nz, rows, width), BF16),
            vm((n, 1, 128), F32),
            vm((n, 1, 128), F32),
            vm((width, hidden), BF16),
            vm((width, hidden), BF16),
            vm((hidden, width), BF16),
            vm((n * rows, hidden), F32),
            vm((n * rows, hidden), F32),
            vm((n * rows, hidden), BF16),
            vm((units, 2, 2, nz, rows, dc), BF16),
            vm((units, 2, nz, rows, dc), BF16),
            vm((units, nz, rows, dc), BF16),
            vm((units, nz, rows, dc), BF16),
            vm((units, nz, rows, dc), BF16),
            vm((units, nz - 1, rows, dc), BF16),
            dma((units, nz - 1)), dma((units, nz - 1)),
            dma((units, nz)), dma((units, nz)),
            dma((units, 2)), dma((units, 2)),
            dma((n - 1,)), dma((n - 1,)),
            dma((units,)), dma((units,)),
            dma((units, nz)), dma((units, nz)),
            dma((units, nz - 1)), dma((units, nz - 1)),
            dma((3, CHUNKS)), dma,
        ],
        compiler_params=pltpu.CompilerParams(
            collective_id=0, has_side_effects=True, vmem_limit_bytes=67000000
        ),
    )(x, ids, probs, flags, wg, wu, wd)


def on_device(hidden_states, expert_ids, router_probs, swap_flags, w_gate, w_up, w_down):
    n = lax.axis_size("expert")
    return moe(n, hidden_states, expert_ids, router_probs, swap_flags, w_gate, w_up, w_down)


def solution(mesh):
    return jax.shard_map(
        on_device,
        mesh=mesh,
        in_specs=(
            P(None, ("groups", "expert"), None),
            P(None, ("groups", "expert"), None),
            P(None, ("groups", "expert"), None),
            P(),
            P("expert", None, None),
            P("expert", None, None),
            P("expert", None, None),
        ),
        out_specs=P(None, ("groups", "expert"), None),
        check_vma=False,
    )
```
